32 devices in a mesh: slab: 16 (over z, x, core), tpl: 2 (over y).
Axes of the slice: x: 2, y: 2, z: 4, core: 2. Of those that a mesh axis runs over, the one named last changes fastest.
Arguments:
- data: bfloat16 [128, 3, 16384], P('tpl', None, 'slab')
- templates: bfloat16 [64, 8, 3, 512], P(('tpl', 'slab')), may hold values from -6 to 6
- stations: int32 [64, 8], P(('tpl', 'slab')), may hold values from 0 to 127
- shifts: int32 [64, 8], P(('tpl', 'slab')), may hold values from 0 to 255
- used: int32 [64], P(('tpl', 'slab')), may hold values from 1 to 8
Outputs:
- detection: float32 [64, 16384], P('tpl', 'slab')
The draws below stay inside these ranges and needn't reach their ends.
Inputs may be any that keep to these rules, and one draw needn't show every extreme that they name: Only the first used[j] slots of template j count; stations may repeat.
All inputs are finite; a program needn't handle non-finite values.
Results may differ from the reference program's by a relative error of at most 0.0065.
Values may be sent and summed in bfloat16 or wider, within the bound.
A program may use at most 256 MiB of HBM per device.

```python
import math
import jax
import jax.numpy as jnp
from jax import lax

COMP = 3
L = 512
K = 8
MAXSHIFT = 256
STA = 128
NS = 16384
NT = 64
RIM = 768


def draw_data(key, part):
    first, second, third = jax.random.split(key, 3)
    base = jax.random.normal(first, (STA, COMP, NS), jnp.float32)
    top = math.log(10.0)
    station_scale = jnp.exp(jax.random.uniform(second, (STA, 1, 1), jnp.float32, 0.0, math.log(10.0)))
    block_scale = jnp.exp(jax.random.uniform(third, (1, 1, NS // 32), jnp.float32, 0.0, top))
    time_scale = jnp.repeat(block_scale, 32, axis=2)
    return (base * station_scale * time_scale).astype(jnp.bfloat16)


def with_ends(array, stream_key, low, largest):
    shape = array.shape
    index_at = [jax.random.randint(jax.random.fold_in(stream_key, axis), (), 0, shape[axis]) for axis in range(len(shape))]
    array = array.at[tuple(index_at)].set(low)
    longest = shape.index(max(shape))
    index_at[longest] = (index_at[longest] + 1) % shape[longest]
    return array.at[tuple(index_at)].set(largest)


def level_of(key, shape, cuts, smallest, top_value):
    factor_of = 1.0
    for dim, shards_of in cuts:
        heights = jax.random.uniform(jax.random.fold_in(jax.random.fold_in(key, 6), dim), (shards_of,), jnp.float32, smallest / len(cuts), top_value / len(cuts))
        factor_of = factor_of * jnp.repeat(jnp.exp(heights), shape[dim] // shards_of).reshape((-1,) + (1,) * (len(shape) - 1 - dim))
    return factor_of


def centred(stream_key, dims, width, most, cuts=(), kind=jnp.bfloat16):
    values = jax.random.normal(stream_key, dims, jnp.float32) * width
    if len(cuts) > 0:
        values = level_of(stream_key, dims, cuts, -0.22, 0.18) * values
    return jnp.clip(values, min=-most, max=most).astype(kind)


def setup_inputs(seed: int = 0) -> dict:
    splits = jax.random.split(jax.random.key(seed), 6)
    data = draw_data(jax.random.fold_in(splits[5], 71), 0)
    templates = centred(splits[1], (NT, K, COMP, L), 1.0, 6.0, ((0, 32),))
    stations = with_ends(jax.random.randint(splits[2], (NT, K), 0, STA), jax.random.fold_in(splits[2], 1), 0, STA - 1).astype(jnp.int32)
    shifts = with_ends(jax.random.randint(splits[3], (NT, K), 0, MAXSHIFT), jax.random.fold_in(splits[3], 1), 0, MAXSHIFT - 1).astype(jnp.int32)
    used = with_ends(jax.random.randint(splits[4], (NT,), 1, K + 1), jax.random.fold_in(splits[4], 1), 1, K).astype(jnp.int32)
    return dict(data=data, templates=templates, stations=stations, shifts=shifts, used=used)


EPS = 1e-05

def normalize(templates):
    span = templates.shape[-1]
    rows = templates.astype(jnp.float32)
    centered = rows - lax.optimization_barrier(jnp.mean(rows, axis=-1, keepdims=True))
    rms = jnp.sqrt(lax.optimization_barrier(jnp.mean(centered * centered, axis=-1, keepdims=True)) + EPS)
    return (centered / (rms * math.sqrt(span))).astype(jnp.bfloat16)

def reference(data, templates, stations, shifts, used):
    total = data.shape[2]
    length = total + RIM
    extended = jnp.pad(data.astype(jnp.float32), ((0, 0), (0, 0), (0, RIM)))
    spectrum = jnp.fft.rfft(extended, n=length, axis=-1)
    ones_f = jnp.conj(jnp.fft.rfft(jnp.ones((L,), jnp.float32), n=length))
    keep = total + MAXSHIFT
    sums = jnp.fft.irfft(spectrum * ones_f, n=length, axis=-1)[..., :keep]
    squares = jnp.fft.irfft(jnp.fft.rfft(extended * extended, n=length, axis=-1) * ones_f, n=length, axis=-1)[..., :keep]
    spread = (squares - sums * sums / L) / L
    inv_norm = (1.0 / (math.sqrt(L) * jnp.sqrt(jnp.maximum(spread, 0.0) + EPS))).astype(jnp.bfloat16)
    unit = normalize(templates)

    def one(item):
        tn, sta, sh, count = item
        rows = spectrum[sta]
        tf = jnp.conj(jnp.fft.rfft(tn.astype(jnp.float32), n=length, axis=-1))
        full = jnp.fft.irfft(rows * tf, n=length, axis=-1)
        corr = jax.vmap(lambda r, s: lax.dynamic_slice_in_dim(r, s, total, 1))(full, sh)
        norms = jax.vmap(lambda r, s: lax.dynamic_slice_in_dim(r, s, total, 1))(inv_norm[sta], sh)
        slots = jnp.arange(K, dtype=jnp.int32)
        scale = jnp.sqrt(L / (3.0 * count.astype(jnp.float32)))
        weight = jnp.where(slots < count, scale, 0.0).astype(jnp.float32)
        return lax.optimization_barrier(jnp.sum(corr * norms.astype(jnp.float32) * weight[:, None, None], axis=(0, 1)))
    return lax.map(one, (unit, stations, shifts, used))
```

```python
import functools
import math

import jax
import jax.numpy as jnp
from jax import lax
from jax.experimental import pallas as pl
from jax.experimental.pallas import tpu as pltpu
from jax.sharding import PartitionSpec as P

MAXSHIFT = 256


EPS = 1e-05


def passed_along(value, axis, steps):
    count = lax.axis_size(axis)
    initial, last = (max(0, -steps), min(count, count - steps))
    return lax.ppermute(value, axis, [(source, source + steps) for source in range(initial, last)])


def normalize(templates):
    span = templates.shape[-1]
    rows = templates.astype(jnp.float32)
    centered = rows - jnp.mean(rows, axis=-1, keepdims=True)
    rms = jnp.sqrt(jnp.mean(centered * centered, axis=-1, keepdims=True) + EPS)
    return (centered / (rms * math.sqrt(span))).astype(jnp.bfloat16)


LANES = 128
STEP = 32
TURNS = LANES // STEP
GROUP = 8
PLANE = 16


def prepare(span, ext_ref, xs_ref, ns_ref, sums_rows):
    rows, width = ext_ref.shape
    block = 256
    reach = block + span
    taps = lax.broadcasted_iota(jnp.int32, (reach, block), 0)
    starts = lax.broadcasted_iota(jnp.int32, (reach, block), 1)
    band = jnp.where((taps >= starts) & (taps < starts + span), 1.0, 0.0).astype(jnp.bfloat16)
    nblocks = (width - span) // block
    root = math.sqrt(span)

    @pl.loop(0, rows // sums_rows)
    def _(step):
        at = pl.ds(pl.multiple_of(step * sums_rows, sums_rows), sums_rows)
        for row in range(width // LANES):
            xs_ref[at, row, :] = ext_ref[at, row * LANES : (row + 1) * LANES].astype(jnp.float32)
        for row in range(width // LANES, PLANE):
            xs_ref[at, row, :] = jnp.zeros((sums_rows, LANES), jnp.float32)
        for n in range(nblocks):
            values = ext_ref[at, n * block : n * block + reach]
            wide = values.astype(jnp.float32)
            square = wide * wide
            high = square.astype(jnp.bfloat16)
            low = (square - high.astype(jnp.float32)).astype(jnp.bfloat16)
            sums = jnp.dot(values, band, preferred_element_type=jnp.float32)
            squares = jnp.dot(high, band, preferred_element_type=jnp.float32)
            squares += jnp.dot(low, band, preferred_element_type=jnp.float32)
            spread = (squares - sums * sums / span) / span
            inverse = 1.0 / (root * jnp.sqrt(jnp.maximum(spread, 0.0) + EPS))
            inverse = inverse.astype(jnp.bfloat16).astype(jnp.float32)
            for half in range(block // LANES):
                ns_ref[at, n * (block // LANES) + half, :] = inverse[:, half * LANES : (half + 1) * LANES]


def kernel(span, chans, row_ref, shift_ref, live_ref, scale_ref, ext_ref, unit_ref, out_ref, xs_ref, ns_ref, left_ref, right_ref):
    prepare(span, ext_ref, xs_ref, ns_ref, 128)
    panel = out_ref.shape[0]
    parts = span // LANES
    lane = lax.broadcasted_iota(jnp.int32, (8, LANES), 1)
    lane_wide = lax.broadcasted_iota(jnp.int32, (STEP, LANES), 1)
    lag = lax.broadcasted_iota(jnp.int32, (STEP, LANES), 0)
    inside = lane_wide >= lag
    lane_part = lane // STEP
    zero_step = jnp.zeros((STEP, LANES), jnp.float32)

    def template(j, _):
        live = live_ref[j]

        def group(g, total):
            base = j * chans + g * GROUP
            for i in range(GROUP):
                index = base + i
                row = row_ref[index]
                shift = shift_ref[index]
                turned = []
                for part in range(parts):
                    line = jnp.broadcast_to(unit_ref[pl.ds(index * parts + part, 1), :], (STEP, LANES))
                    turned.append(pltpu.roll(line, 0, 1, stride=1, stride_axis=0))
                edges = [zero_step] + turned + [zero_step]
                for part in range(parts + 1):
                    piece = jnp.where(inside, edges[part + 1], edges[part])
                    right_ref[i * STEP : (i + 1) * STEP, part * LANES : (part + 1) * LANES] = piece.astype(jnp.bfloat16)
                lines = []
                for turn in range(TURNS):
                    offset = shift + STEP * turn
                    first = offset // LANES
                    rest = offset % LANES
                    keep = lane >= rest
                    loads = [xs_ref[row, pl.ds(first + part, 8), :] for part in range(parts + 2)]
                    lines.append([
                        pltpu.roll(jnp.where(keep, loads[part], loads[part + 1]), LANES - rest, 1)
                        for part in range(parts + 1)
                    ])
                for part in range(parts + 1):
                    for pair in range(TURNS // 2):
                        both = jnp.concatenate([lines[2 * pair][part], lines[2 * pair + 1][part]], axis=0)
                        at = i * STEP + pair * 16
                        left_ref[at : at + 16, part * LANES : (part + 1) * LANES] = both.astype(jnp.bfloat16)
            for four in range(GROUP // TURNS):
                at = slice(four * LANES, (four + 1) * LANES)
                corr = lax.dot_general(
                    left_ref[at, :], right_ref[at, :], (((1,), (1,)), ((), ())),
                    preferred_element_type=jnp.float32,
                )
                for i in range(TURNS):
                    kc = g * GROUP + four * TURNS + i
                    index = j * chans + kc
                    row = row_ref[index]
                    shift = shift_ref[index]
                    wanted = (lane_part == i) & (kc < live)
                    added = []
                    for turn in range(TURNS):
                        offset = shift + STEP * turn
                        first = offset // LANES
                        rest = offset % LANES
                        near = ns_ref[row, pl.ds(first, 8), :]
                        far = ns_ref[row, pl.ds(first + 1, 8), :]
                        norm = pltpu.roll(jnp.where(lane >= rest, near, far), LANES + STEP * i - rest, 1)
                        value = corr[i * STEP + 8 * turn : i * STEP + 8 * turn + 8, :]
                        added.append(jnp.where(wanted, value * norm, 0.0))
                    total = tuple(t + a for t, a in zip(total, added))
            return total

        zero = jnp.zeros((8, LANES), jnp.float32)
        total = lax.fori_loop(0, (live + GROUP - 1) // GROUP, group, (zero,) * TURNS)
        result = zero
        for turn in range(TURNS):
            value = total[turn]
            value = value + pltpu.roll(value, LANES // 2, 1)
            value = value + pltpu.roll(value, LANES // 4, 1)
            result = jnp.where(lane_part == turn, value, result)
        out_ref[j] = result * scale_ref[j]
        return 0

    lax.fori_loop(0, panel, template, 0)


def detect(ext, unit, rows, shifts, live, scale, span, samples):
    chans = unit.shape[0] // live.shape[0]
    smem = pl.BlockSpec(memory_space=pltpu.SMEM)
    vmem = pl.BlockSpec(memory_space=pltpu.VMEM)
    panel = live.shape[0]
    return pl.pallas_call(
        functools.partial(kernel, span, chans),
        out_shape=jax.ShapeDtypeStruct((panel, samples // LANES, LANES), jnp.float32),
        in_specs=[smem, smem, smem, smem, vmem, vmem],
        out_specs=vmem,
        scratch_shapes=[
            pltpu.VMEM((ext.shape[0], PLANE, LANES), jnp.float32),
            pltpu.VMEM((ext.shape[0], PLANE, LANES), jnp.float32),
            pltpu.VMEM((GROUP * STEP, span + LANES), jnp.bfloat16),
            pltpu.VMEM((GROUP * STEP, span + LANES), jnp.bfloat16),
        ],
        compiler_params=pltpu.CompilerParams(vmem_limit_bytes=56 << 20),
    )(rows, shifts, live, scale, ext, unit.reshape(-1, LANES).astype(jnp.float32))


def per_device(data, templates, stations, shifts, used):
    span = templates.shape[3]
    comps = data.shape[1]
    samples = data.shape[2]
    reach = span + MAXSHIFT
    local = data.reshape(-1, samples)
    whole = lax.all_gather(local, "tpl", axis=0, tiled=True)
    tail = passed_along(whole[:, :reach], "slab", -1)
    extended = jnp.concatenate([whole, tail], axis=1)
    slots = templates.shape[1]
    unit = normalize(templates).reshape(-1, span)
    tn = lax.all_gather(unit, "slab", axis=0, tiled=True)
    lists = jnp.concatenate([stations, shifts, used[:, None]], axis=1)
    lists = lax.all_gather(lists, "slab", axis=0, tiled=True)
    sta = lists[:, :slots]
    sh = lists[:, slots : 2 * slots]
    count = lists[:, 2 * slots]
    rows = (sta[:, :, None] * comps + jnp.arange(comps, dtype=jnp.int32)).reshape(-1)
    moves = jnp.repeat(sh.reshape(-1), comps)
    scale = jnp.sqrt(span / (3.0 * count.astype(jnp.float32)))
    stack = detect(extended, tn, rows, moves, count * comps, scale, span, samples)
    return stack.reshape(-1, samples)


def solution(mesh):
    return jax.shard_map(
        per_device,
        mesh=mesh,
        in_specs=(
            P("tpl", None, "slab"),
            P(("tpl", "slab"), None, None, None),
            P(("tpl", "slab"), None),
            P(("tpl", "slab"), None),
            P(("tpl", "slab")),
        ),
        out_specs=P("tpl", "slab"),
        check_vma=False,
    )
```

```python
import functools
import math

import jax
import jax.numpy as jnp
from jax import lax
from jax.experimental import pallas as pl
from jax.experimental.pallas import tpu as pltpu
from jax.sharding import PartitionSpec as P

MAXSHIFT = 256


EPS = 1e-05
MESH = pl.DeviceIdType.MESH


def normalize(templates):
    span = templates.shape[-1]
    rows = templates.astype(jnp.float32)
    centered = rows - jnp.mean(rows, axis=-1, keepdims=True)
    rms = jnp.sqrt(jnp.mean(centered * centered, axis=-1, keepdims=True) + EPS)
    return (centered / (rms * math.sqrt(span))).astype(jnp.bfloat16)


LANES = 128
STEP = 32
TURNS = LANES // STEP
GROUP = 8
PLANE = 16


def prepare(span, ext_ref, xs_ref, ns_ref, sums_rows):
    rows, width = ext_ref.shape
    block = 256
    reach = block + span
    taps = lax.broadcasted_iota(jnp.int32, (reach, block), 0)
    starts = lax.broadcasted_iota(jnp.int32, (reach, block), 1)
    band = jnp.where((taps >= starts) & (taps < starts + span), 1.0, 0.0).astype(jnp.bfloat16)
    nblocks = (width - span) // block
    root = math.sqrt(span)

    @pl.loop(0, rows // sums_rows)
    def _(step):
        at = pl.ds(pl.multiple_of(step * sums_rows, sums_rows), sums_rows)
        for row in range(width // LANES):
            xs_ref[at, row, :] = ext_ref[at, row * LANES : (row + 1) * LANES].astype(jnp.float32)
        for row in range(width // LANES, PLANE):
            xs_ref[at, row, :] = jnp.zeros((sums_rows, LANES), jnp.float32)
        for n in range(nblocks):
            values = ext_ref[at, n * block : n * block + reach]
            wide = values.astype(jnp.float32)
            square = wide * wide
            high = square.astype(jnp.bfloat16)
            low = (square - high.astype(jnp.float32)).astype(jnp.bfloat16)
            sums = jnp.dot(values, band, preferred_element_type=jnp.float32)
            squares = jnp.dot(high, band, preferred_element_type=jnp.float32)
            squares += jnp.dot(low, band, preferred_element_type=jnp.float32)
            spread = (squares - sums * sums / span) / span
            inverse = 1.0 / (root * jnp.sqrt(jnp.maximum(spread, 0.0) + EPS))
            inverse = inverse.astype(jnp.bfloat16).astype(jnp.float32)
            for half in range(block // LANES):
                ns_ref[at, n * (block // LANES) + half, :] = inverse[:, half * LANES : (half + 1) * LANES]


def kernel(span, chans, mine, height, table_ref, ext_ref, panels_ref, out_ref, xs_ref, ns_ref, unit_ref, left_ref, right_ref):
    prepare(span, ext_ref, xs_ref, ns_ref, 128)
    panel = out_ref.shape[0]
    parts = span // LANES

    @pl.loop(0, panels_ref.shape[0] // height)
    def _(step):
        at = pl.ds(pl.multiple_of(step * height, height), height)
        for part in range(parts):
            unit_ref[part, at, :] = panels_ref[at, part * LANES : (part + 1) * LANES].astype(jnp.float32)

    lane = lax.broadcasted_iota(jnp.int32, (8, LANES), 1)
    lane_wide = lax.broadcasted_iota(jnp.int32, (STEP, LANES), 1)
    lag = lax.broadcasted_iota(jnp.int32, (STEP, LANES), 0)
    inside = lane_wide >= lag
    lane_part = lane // STEP
    zero_step = jnp.zeros((STEP, LANES), jnp.float32)

    def template(j, _):
        live = table_ref[2 * panel * chans + j]
        origin = (j // mine) * height + lax.rem(j, mine) * chans

        def group(g, total):
            base = j * chans + g * GROUP
            for i in range(GROUP):
                index = base + i
                row = table_ref[index]
                shift = table_ref[panel * chans + index]
                turned = []
                for part in range(parts):
                    line = jnp.broadcast_to(unit_ref[part, pl.ds(origin + g * GROUP + i, 1), :], (STEP, LANES))
                    turned.append(pltpu.roll(line, 0, 1, stride=1, stride_axis=0))
                edges = [zero_step] + turned + [zero_step]
                for part in range(parts + 1):
                    piece = jnp.where(inside, edges[part + 1], edges[part])
                    right_ref[i * STEP : (i + 1) * STEP, part * LANES : (part + 1) * LANES] = piece.astype(jnp.bfloat16)
                lines = []
                for turn in range(TURNS):
                    offset = shift + STEP * turn
                    first = offset // LANES
                    rest = offset % LANES
                    keep = lane >= rest
                    loads = [xs_ref[row, pl.ds(first + part, 8), :] for part in range(parts + 2)]
                    lines.append([
                        pltpu.roll(jnp.where(keep, loads[part], loads[part + 1]), LANES - rest, 1)
                        for part in range(parts + 1)
                    ])
                for part in range(parts + 1):
                    for pair in range(TURNS // 2):
                        both = jnp.concatenate([lines[2 * pair][part], lines[2 * pair + 1][part]], axis=0)
                        at = i * STEP + pair * 16
                        left_ref[at : at + 16, part * LANES : (part + 1) * LANES] = both.astype(jnp.bfloat16)
            for four in range(GROUP // TURNS):
                at = slice(four * LANES, (four + 1) * LANES)
                corr = lax.dot_general(
                    left_ref[at, :], right_ref[at, :], (((1,), (1,)), ((), ())),
                    preferred_element_type=jnp.float32,
                )
                for i in range(TURNS):
                    kc = g * GROUP + four * TURNS + i
                    index = j * chans + kc
                    row = table_ref[index]
                    shift = table_ref[panel * chans + index]
                    wanted = (lane_part == i) & (kc < live)
                    added = []
                    for turn in range(TURNS):
                        offset = shift + STEP * turn
                        first = offset // LANES
                        rest = offset % LANES
                        near = ns_ref[row, pl.ds(first, 8), :]
                        far = ns_ref[row, pl.ds(first + 1, 8), :]
                        norm = pltpu.roll(jnp.where(lane >= rest, near, far), LANES + STEP * i - rest, 1)
                        value = corr[i * STEP + 8 * turn : i * STEP + 8 * turn + 8, :]
                        added.append(jnp.where(wanted, value * norm, 0.0))
                    total = tuple(t + a for t, a in zip(total, added))
            return total

        zero = jnp.zeros((8, LANES), jnp.float32)
        total = lax.fori_loop(0, (live + GROUP - 1) // GROUP, group, (zero,) * TURNS)
        result = zero
        for turn in range(TURNS):
            value = total[turn]
            value = value + pltpu.roll(value, LANES // 2, 1)
            value = value + pltpu.roll(value, LANES // 4, 1)
            result = jnp.where(lane_part == turn, value, result)
        used3 = jnp.full((8, LANES), live, jnp.int32).astype(jnp.float32)
        out_ref[j] = result * jnp.sqrt(span / used3)
        return 0

    lax.fori_loop(0, panel, template, 0)


def detect(ext, panels, table, panel, mine, chans, height, span, samples):
    smem = pl.BlockSpec(memory_space=pltpu.SMEM)
    vmem = pl.BlockSpec(memory_space=pltpu.VMEM)
    return pl.pallas_call(
        functools.partial(kernel, span, chans, mine, height),
        out_shape=jax.ShapeDtypeStruct((panel, samples // LANES, LANES), jnp.float32),
        in_specs=[smem, vmem, vmem],
        out_specs=vmem,
        scratch_shapes=[
            pltpu.VMEM((ext.shape[0], PLANE, LANES), jnp.float32),
            pltpu.VMEM((ext.shape[0], PLANE, LANES), jnp.float32),
            pltpu.VMEM((span // LANES, panels.shape[0], LANES), jnp.float32),
            pltpu.VMEM((GROUP * STEP, span + LANES), jnp.bfloat16),
            pltpu.VMEM((GROUP * STEP, span + LANES), jnp.bfloat16),
        ],
        compiler_params=pltpu.CompilerParams(vmem_limit_bytes=56 << 20),
    )(table, ext, panels)


def exchange_kernel(reach, data_ref, panel_ref, ext_ref, panels_ref, *sems):
    near_send, near_recv, far_send, far_recv, halo_send, halo_recv = sems[:6]
    wide_send, wide_recv, mate_send, mate_recv = sems[6:]
    rows, samples = data_ref.shape
    height = panel_ref.shape[0]
    slabs = lax.axis_size("slab")
    blocks = lax.axis_size("tpl")
    pairs = slabs // 2
    slab = lax.axis_index("slab")
    tpl = lax.axis_index("tpl")
    mate = slab + 1 - 2 * lax.rem(slab, 2)

    barrier = pltpu.get_barrier_semaphore()
    for d in range(1, blocks):
        pl.semaphore_signal(barrier, inc=1, device_id={"tpl": lax.rem(tpl + d, blocks)}, device_id_type=MESH)
    for d in range(1, slabs):
        pl.semaphore_signal(barrier, inc=1, device_id={"slab": lax.rem(slab + d, slabs)}, device_id_type=MESH)
    pl.semaphore_wait(barrier, blocks + slabs - 2)

    def group(t):
        return pl.ds(pl.multiple_of(t * rows, rows), rows)

    def place(p):
        return pl.ds(pl.multiple_of(p * height, height), height)

    def near_copy(d):
        return pltpu.make_async_remote_copy(
            src_ref=data_ref.at[:, :reach], dst_ref=ext_ref.at[group(tpl), :reach],
            send_sem=near_send.at[d], recv_sem=near_recv.at[d],
            device_id={"tpl": lax.rem(tpl + d, blocks)}, device_id_type=MESH)

    def far_copy(d):
        return pltpu.make_async_remote_copy(
            src_ref=data_ref.at[:, reach:], dst_ref=ext_ref.at[group(tpl), reach:samples],
            send_sem=far_send.at[d], recv_sem=far_recv.at[d],
            device_id={"tpl": lax.rem(tpl + d, blocks)}, device_id_type=MESH)

    def halo_copy(d):
        source = data_ref.at[:, :reach]
        if d > 0:
            source = ext_ref.at[group(lax.rem(tpl + blocks - d, blocks)), :reach]
        return pltpu.make_async_remote_copy(
            src_ref=source, dst_ref=ext_ref.at[group(lax.rem(tpl + blocks - d, blocks)), samples:],
            send_sem=halo_send.at[d], recv_sem=halo_recv.at[d],
            device_id={"slab": lax.rem(slab + slabs - 1, slabs)}, device_id_type=MESH)

    def wide_copy(d):
        return pltpu.make_async_remote_copy(
            src_ref=panel_ref, dst_ref=panels_ref.at[place(slab), :],
            send_sem=wide_send.at[d], recv_sem=wide_recv.at[d],
            device_id={"slab": lax.rem(slab + 2 * d, slabs)}, device_id_type=MESH)

    def mate_copy(d):
        source = panel_ref
        if d > 0:
            source = panels_ref.at[place(lax.rem(slab + slabs - 2 * d, slabs)), :]
        return pltpu.make_async_remote_copy(
            src_ref=source, dst_ref=panels_ref.at[place(lax.rem(slab + slabs - 2 * d, slabs)), :],
            send_sem=mate_send.at[d], recv_sem=mate_recv.at[d],
            device_id={"slab": mate}, device_id_type=MESH)

    first = slab == 0
    last = slab == slabs - 1
    for d in range(1, blocks):
        near_copy(d).start()
    for d in range(1, pairs):
        wide_copy(d).start()
    for d in range(1, blocks):
        far_copy(d).start()
    mate_copy(0).start()

    @pl.when(jnp.logical_not(first))
    def _():
        halo_copy(0).start()

    ext_ref[group(tpl), :samples] = data_ref[...]
    panels_ref[place(slab), :] = panel_ref[...]

    @pl.when(last)
    def _():
        ext_ref[:, samples:] = jnp.zeros((rows * blocks, reach), ext_ref.dtype)

    for d in range(1, pairs):
        wide_copy(d).wait_recv()
        mate_copy(d).start()
    for d in range(1, blocks):
        near_copy(d).wait_recv()

        @pl.when(jnp.logical_not(first))
        def _():
            halo_copy(d).start()

    for d in range(1, blocks):
        far_copy(d).wait_recv()
        near_copy(d).wait_send()
        far_copy(d).wait_send()
    for d in range(1, pairs):
        wide_copy(d).wait_send()
    for d in range(pairs):
        mate_copy(d).wait_recv()
        mate_copy(d).wait_send()

    @pl.when(jnp.logical_not(first))
    def _():
        for d in range(blocks):
            halo_copy(d).wait_send()

    @pl.when(jnp.logical_not(last))
    def _():
        for d in range(blocks):
            halo_copy(d).wait_recv()


def exchange(local, panel, reach):
    slabs = lax.axis_size("slab")
    blocks = lax.axis_size("tpl")
    rows, samples = local.shape
    height, span = panel.shape
    vmem = pl.BlockSpec(memory_space=pltpu.VMEM)
    dma = pltpu.SemaphoreType.DMA
    return pl.pallas_call(
        functools.partial(exchange_kernel, reach),
        out_shape=(
            jax.ShapeDtypeStruct((rows * blocks, samples + reach), local.dtype),
            jax.ShapeDtypeStruct((height * slabs, span), panel.dtype),
        ),
        in_specs=[vmem, vmem],
        out_specs=(vmem, vmem),
        scratch_shapes=[dma((blocks,))] * 6 + [dma((slabs // 2,))] * 4,
        compiler_params=pltpu.CompilerParams(
            collective_id=0, has_side_effects=True, vmem_limit_bytes=40 << 20
        ),
    )(local, panel)


def per_device(data, templates, stations, shifts, used):
    span = templates.shape[3]
    comps = data.shape[1]
    samples = data.shape[2]
    reach = span + MAXSHIFT
    slots = templates.shape[1]
    mine = templates.shape[0]
    local = data.reshape(-1, samples)
    unit = normalize(templates).reshape(-1, span)
    lists = jnp.concatenate(
        [stations.reshape(-1) // 256, stations.reshape(-1) % 256, shifts.reshape(-1), used]
    )
    lists = jnp.pad(lists.astype(jnp.bfloat16), (0, span - lists.shape[0]))
    lists = jnp.pad(lists[None], ((0, 15), (0, 0)))
    extended, panels = exchange(local, jnp.concatenate([unit, lists], axis=0), reach)
    slabs = lax.axis_size("slab")
    height = unit.shape[0] + 16
    each = mine * slots
    got = panels.reshape(slabs, height, span)[:, unit.shape[0], : 3 * each + mine].astype(jnp.int32)
    sta = got[:, :each] * 256 + got[:, each : 2 * each]
    rows = (sta[:, :, None] * comps + jnp.arange(comps, dtype=jnp.int32)).reshape(-1)
    moves = jnp.repeat(got[:, 2 * each : 3 * each].reshape(-1), comps)
    live = got[:, 3 * each :].reshape(-1) * comps
    table = jnp.concatenate([rows, moves, live])
    stack = detect(extended, panels, table, mine * slabs, mine, slots * comps, height, span, samples)
    return stack.reshape(-1, samples)


def solution(mesh):
    return jax.shard_map(
        per_device,
        mesh=mesh,
        in_specs=(
            P("tpl", None, "slab"),
            P(("tpl", "slab"), None, None, None),
            P(("tpl", "slab"), None),
            P(("tpl", "slab"), None),
            P(("tpl", "slab")),
        ),
        out_specs=P("tpl", "slab"),
        check_vma=False,
    )
```

```python
import functools
import math

import jax
import jax.numpy as jnp
from jax import lax
from jax.experimental import pallas as pl
from jax.experimental.pallas import tpu as pltpu
from jax.sharding import PartitionSpec as P

MAXSHIFT = 256


EPS = 1e-05
MESH = pl.DeviceIdType.MESH


def normalize(templates):
    span = templates.shape[-1]
    rows = templates.astype(jnp.float32)
    centered = rows - jnp.mean(rows, axis=-1, keepdims=True)
    rms = jnp.sqrt(jnp.mean(centered * centered, axis=-1, keepdims=True) + EPS)
    return (centered / (rms * math.sqrt(span))).astype(jnp.bfloat16)


LANES = 128
STEP = 32
TURNS = LANES // STEP
PASS = 4
ROWS = 384
PLANE = 16


def prepare(span, ext_ref, xs_ref, ns_ref, sums_rows):
    rows, width = ext_ref.shape
    block = 256
    reach = block + span
    taps = lax.broadcasted_iota(jnp.int32, (reach, block), 0)
    starts = lax.broadcasted_iota(jnp.int32, (reach, block), 1)
    band = jnp.where((taps >= starts) & (taps < starts + span), 1.0, 0.0).astype(jnp.bfloat16)
    nblocks = (width - span) // block
    root = math.sqrt(span)

    @pl.loop(0, rows // sums_rows)
    def _(step):
        at = pl.ds(pl.multiple_of(step * sums_rows, sums_rows), sums_rows)
        base = pl.multiple_of(step * sums_rows * PLANE, sums_rows * PLANE)
        for row in range(width // LANES):
            xs_ref[pl.ds(base + row, sums_rows, stride=PLANE), :] = ext_ref[at, row * LANES : (row + 1) * LANES].astype(jnp.float32)
        for row in range(width // LANES, PLANE):
            xs_ref[pl.ds(base + row, sums_rows, stride=PLANE), :] = jnp.zeros((sums_rows, LANES), jnp.float32)
        for n in range(nblocks):
            values = ext_ref[at, n * block : n * block + reach]
            wide = values.astype(jnp.float32)
            square = wide * wide
            high = square.astype(jnp.bfloat16)
            low = (square - high.astype(jnp.float32)).astype(jnp.bfloat16)
            sums = jnp.dot(values, band, preferred_element_type=jnp.float32)
            squares = jnp.dot(high, band, preferred_element_type=jnp.float32)
            squares += jnp.dot(low, band, preferred_element_type=jnp.float32)
            spread = (squares - sums * sums / span) / span
            inverse = 1.0 / (root * jnp.sqrt(jnp.maximum(spread, 0.0) + EPS))
            inverse = inverse.astype(jnp.bfloat16).astype(jnp.float32)
            for half in range(block // LANES):
                ns_ref[pl.ds(base + n * (block // LANES) + half, sums_rows, stride=PLANE), :] = inverse[:, half * LANES : (half + 1) * LANES]


def kernel(span, comps, mine, height, slots, table_ref, ext_ref, panels_ref, out_ref, xs_ref, ns_ref, unit_ref, left_ref, right_ref, sum_ref, item_ref, where_ref, line_ref):
    prepare(span, ext_ref, xs_ref, ns_ref, ROWS)
    panel = out_ref.shape[0]
    parts = span // LANES
    count = panel * slots

    @pl.loop(0, panels_ref.shape[0] // height)
    def _(step):
        at = pl.ds(pl.multiple_of(step * height, height), height)
        for part in range(parts):
            unit_ref[part, at, :] = panels_ref[at, part * LANES : (part + 1) * LANES].astype(jnp.float32)

    def collect(j, total):
        origin = (j // mine) * height + lax.rem(j, mine) * slots * comps
        base = j * slots

        def one(k, _):
            item_ref[total + k] = base + k
            where_ref[total + k] = j
            line_ref[total + k] = origin + k * comps
            return 0

        live = table_ref[2 * count + j]
        lax.fori_loop(0, live, one, 0)
        sum_ref[j] = jnp.zeros((STEP, LANES), jnp.float32)
        return total + live

    live_slots = lax.fori_loop(0, panel, collect, 0)
    for k in range(PASS - 1):
        item_ref[live_slots + k] = 0
        where_ref[live_slots + k] = panel
        line_ref[live_slots + k] = 0
    sum_ref[panel] = jnp.zeros((STEP, LANES), jnp.float32)

    lane = lax.broadcasted_iota(jnp.int32, (8, LANES), 1)
    lane_wide = lax.broadcasted_iota(jnp.int32, (STEP, LANES), 1)
    lag = lax.broadcasted_iota(jnp.int32, (STEP, LANES), 0)
    inside = lane_wide >= lag
    lane_part = lax.shift_right_logical(lane, 5)
    zero_step = jnp.zeros((STEP, LANES), jnp.float32)
    zero = jnp.zeros((8, LANES), jnp.float32)

    def body(g, _):
        places = []
        for n in range(PASS):
            item = item_ref[g * PASS + n]
            offsets = [table_ref[count + item] + STEP * turn for turn in range(TURNS)]
            firsts = [lax.shift_right_logical(offset, 7) + table_ref[item] * PLANE for offset in offsets]
            rests = [lax.bitwise_and(offset, LANES - 1) for offset in offsets]
            places.append((firsts, rests, line_ref[g * PASS + n]))
        for quad in range(PASS * comps // TURNS):
            for p in range(TURNS):
                n, c = divmod(quad * TURNS + p, comps)
                firsts, rests, origin = places[n]
                i = quad * TURNS + p
                turned = []
                for part in range(parts):
                    line = jnp.broadcast_to(unit_ref[part, pl.ds(origin + c, 1), :], (STEP, LANES))
                    turned.append(pltpu.roll(line, 0, 1, stride=1, stride_axis=0))
                edges = [zero_step] + turned + [zero_step]
                for part in range(parts + 1):
                    piece = jnp.where(inside, edges[part + 1], edges[part])
                    right_ref[i * STEP : (i + 1) * STEP, part * LANES : (part + 1) * LANES] = piece.astype(jnp.bfloat16)
                lines = []
                for turn in range(TURNS):
                    keep = lane >= rests[turn]
                    back = lax.bitwise_and(LANES - rests[turn], LANES - 1)
                    loads = [xs_ref[pl.ds(firsts[turn] + c * PLANE + part, 8), :] for part in range(parts + 2)]
                    lines.append([
                        pltpu.roll(jnp.where(keep, loads[part], loads[part + 1]), back, 1)
                        for part in range(parts + 1)
                    ])
                for part in range(parts + 1):
                    for pair in range(TURNS // 2):
                        both = jnp.concatenate([lines[2 * pair][part], lines[2 * pair + 1][part]], axis=0)
                        at = i * STEP + pair * 16
                        left_ref[at : at + 16, part * LANES : (part + 1) * LANES] = both.astype(jnp.bfloat16)
        products = []
        for quad in range(PASS * comps // TURNS):
            at = slice(quad * LANES, (quad + 1) * LANES)
            products.append(lax.dot_general(
                left_ref[at, :], right_ref[at, :], (((1,), (1,)), ((), ())),
                preferred_element_type=jnp.float32,
            ))
        for n in range(PASS):
            firsts, rests, _ = places[n]
            added = []
            for turn in range(TURNS):
                value = zero
                for c in range(comps):
                    quad, p = divmod(n * comps + c, TURNS)
                    near = ns_ref[pl.ds(firsts[turn] + c * PLANE, 8), :]
                    far = ns_ref[pl.ds(firsts[turn] + c * PLANE + 1, 8), :]
                    back = lax.bitwise_and(LANES + STEP * p - rests[turn], LANES - 1)
                    norm = pltpu.roll(jnp.where(lane >= rests[turn], near, far), back, 1)
                    corr = products[quad][p * STEP + 8 * turn : p * STEP + 8 * turn + 8, :]
                    value = jnp.where(lane_part == p, corr * norm, value)
                added.append(value)
            j = where_ref[g * PASS + n]
            sum_ref[j] += jnp.concatenate(added, axis=0)
        return 0

    lax.fori_loop(0, lax.shift_right_logical(live_slots + PASS - 1, 2), body, 0)

    def finish(j, _):
        value = sum_ref[j]
        value = value + pltpu.roll(value, LANES // 2, 1)
        value = value + pltpu.roll(value, LANES // 4, 1)
        result = zero
        for turn in range(TURNS):
            result = jnp.where(lane_part == turn, value[8 * turn : 8 * turn + 8, :], result)
        used = jnp.full((8, LANES), table_ref[2 * count + j], jnp.int32).astype(jnp.float32)
        out_ref[j] = result * jnp.sqrt(span / (3.0 * used))
        return 0

    lax.fori_loop(0, panel, finish, 0, unroll=4)


def detect(ext, panels, table, panel, mine, slots, comps, height, span, samples):
    smem = pl.BlockSpec(memory_space=pltpu.SMEM)
    vmem = pl.BlockSpec(memory_space=pltpu.VMEM)
    listed = panel * slots + PASS
    return pl.pallas_call(
        functools.partial(kernel, span, comps, mine, height, slots),
        out_shape=jax.ShapeDtypeStruct((panel, samples // LANES, LANES), jnp.float32),
        in_specs=[smem, vmem, vmem],
        out_specs=vmem,
        scratch_shapes=[
            pltpu.VMEM((ext.shape[0] * PLANE, LANES), jnp.float32),
            pltpu.VMEM((ext.shape[0] * PLANE, LANES), jnp.float32),
            pltpu.VMEM((span // LANES, panels.shape[0], LANES), jnp.float32),
            pltpu.VMEM((PASS * comps * STEP, span + LANES), jnp.bfloat16),
            pltpu.VMEM((PASS * comps * STEP, span + LANES), jnp.bfloat16),
            pltpu.VMEM((panel + 1, STEP, LANES), jnp.float32),
            pltpu.SMEM((listed,), jnp.int32),
            pltpu.SMEM((listed,), jnp.int32),
            pltpu.SMEM((listed,), jnp.int32),
        ],
        compiler_params=pltpu.CompilerParams(vmem_limit_bytes=56 << 20),
    )(table, ext, panels)


def exchange_kernel(reach, data_ref, panel_ref, ext_ref, panels_ref, *sems):
    near_send, near_recv, far_send, far_recv, halo_send, halo_recv = sems[:6]
    wide_send, wide_recv, mate_send, mate_recv = sems[6:]
    rows, samples = data_ref.shape
    height = panel_ref.shape[0]
    slabs = lax.axis_size("slab")
    blocks = lax.axis_size("tpl")
    pairs = slabs // 2
    slab = lax.axis_index("slab")
    tpl = lax.axis_index("tpl")
    mate = slab + 1 - 2 * lax.rem(slab, 2)

    barrier = pltpu.get_barrier_semaphore()
    for d in range(1, blocks):
        pl.semaphore_signal(barrier, inc=1, device_id={"tpl": lax.rem(tpl + d, blocks)}, device_id_type=MESH)
    for d in range(1, slabs):
        pl.semaphore_signal(barrier, inc=1, device_id={"slab": lax.rem(slab + d, slabs)}, device_id_type=MESH)
    pl.semaphore_wait(barrier, blocks + slabs - 2)

    def group(t):
        return pl.ds(pl.multiple_of(t * rows, rows), rows)

    def place(p):
        return pl.ds(pl.multiple_of(p * height, height), height)

    def near_copy(d):
        return pltpu.make_async_remote_copy(
            src_ref=data_ref.at[:, :reach], dst_ref=ext_ref.at[group(tpl), :reach],
            send_sem=near_send.at[d], recv_sem=near_recv.at[d],
            device_id={"tpl": lax.rem(tpl + d, blocks)}, device_id_type=MESH)

    def far_copy(d):
        return pltpu.make_async_remote_copy(
            src_ref=data_ref.at[:, reach:], dst_ref=ext_ref.at[group(tpl), reach:samples],
            send_sem=far_send.at[d], recv_sem=far_recv.at[d],
            device_id={"tpl": lax.rem(tpl + d, blocks)}, device_id_type=MESH)

    def halo_copy(d):
        source = data_ref.at[:, :reach]
        if d > 0:
            source = ext_ref.at[group(lax.rem(tpl + blocks - d, blocks)), :reach]
        return pltpu.make_async_remote_copy(
            src_ref=source, dst_ref=ext_ref.at[group(lax.rem(tpl + blocks - d, blocks)), samples:],
            send_sem=halo_send.at[d], recv_sem=halo_recv.at[d],
            device_id={"slab": lax.rem(slab + slabs - 1, slabs)}, device_id_type=MESH)

    def wide_copy(d):
        return pltpu.make_async_remote_copy(
            src_ref=panel_ref, dst_ref=panels_ref.at[place(slab), :],
            send_sem=wide_send.at[d], recv_sem=wide_recv.at[d],
            device_id={"slab": lax.rem(slab + 2 * d, slabs)}, device_id_type=MESH)

    def mate_copy(d):
        source = panel_ref
        if d > 0:
            source = panels_ref.at[place(lax.rem(slab + slabs - 2 * d, slabs)), :]
        return pltpu.make_async_remote_copy(
            src_ref=source, dst_ref=panels_ref.at[place(lax.rem(slab + slabs - 2 * d, slabs)), :],
            send_sem=mate_send.at[d], recv_sem=mate_recv.at[d],
            device_id={"slab": mate}, device_id_type=MESH)

    first = slab == 0
    last = slab == slabs - 1
    for d in range(1, blocks):
        near_copy(d).start()
    for d in range(1, pairs):
        wide_copy(d).start()
    for d in range(1, blocks):
        far_copy(d).start()
    mate_copy(0).start()

    @pl.when(jnp.logical_not(first))
    def _():
        halo_copy(0).start()

    ext_ref[group(tpl), :samples] = data_ref[...]
    panels_ref[place(slab), :] = panel_ref[...]

    @pl.when(last)
    def _():
        ext_ref[:, samples:] = jnp.zeros((rows * blocks, reach), ext_ref.dtype)

    for d in range(1, pairs):
        wide_copy(d).wait_recv()
        mate_copy(d).start()
    for d in range(1, blocks):
        near_copy(d).wait_recv()

        @pl.when(jnp.logical_not(first))
        def _():
            halo_copy(d).start()

    for d in range(1, blocks):
        far_copy(d).wait_recv()
        near_copy(d).wait_send()
        far_copy(d).wait_send()
    for d in range(1, pairs):
        wide_copy(d).wait_send()
    for d in range(pairs):
        mate_copy(d).wait_recv()
        mate_copy(d).wait_send()

    @pl.when(jnp.logical_not(first))
    def _():
        for d in range(blocks):
            halo_copy(d).wait_send()

    @pl.when(jnp.logical_not(last))
    def _():
        for d in range(blocks):
            halo_copy(d).wait_recv()


def exchange(local, panel, reach):
    slabs = lax.axis_size("slab")
    blocks = lax.axis_size("tpl")
    rows, samples = local.shape
    height, span = panel.shape
    vmem = pl.BlockSpec(memory_space=pltpu.VMEM)
    dma = pltpu.SemaphoreType.DMA
    return pl.pallas_call(
        functools.partial(exchange_kernel, reach),
        out_shape=(
            jax.ShapeDtypeStruct((rows * blocks, samples + reach), local.dtype),
            jax.ShapeDtypeStruct((height * slabs, span), panel.dtype),
        ),
        in_specs=[vmem, vmem],
        out_specs=(vmem, vmem),
        scratch_shapes=[dma((blocks,))] * 6 + [dma((slabs // 2,))] * 4,
        compiler_params=pltpu.CompilerParams(
            collective_id=0, has_side_effects=True, vmem_limit_bytes=40 << 20
        ),
    )(local, panel)


def per_device(data, templates, stations, shifts, used):
    span = templates.shape[3]
    comps = data.shape[1]
    samples = data.shape[2]
    reach = span + MAXSHIFT
    slots = templates.shape[1]
    mine = templates.shape[0]
    local = data.reshape(-1, samples)
    unit = normalize(templates).reshape(-1, span)
    lists = jnp.concatenate(
        [stations.reshape(-1) // 256, stations.reshape(-1) % 256, shifts.reshape(-1), used]
    )
    lists = jnp.pad(lists.astype(jnp.bfloat16), (0, span - lists.shape[0]))
    lists = jnp.pad(lists[None], ((0, 15), (0, 0)))
    extended, panels = exchange(local, jnp.concatenate([unit, lists], axis=0), reach)
    slabs = lax.axis_size("slab")
    height = unit.shape[0] + 16
    each = mine * slots
    got = panels.reshape(slabs, height, span)[:, unit.shape[0], : 3 * each + mine].astype(jnp.int32)
    sta = got[:, :each] * 256 + got[:, each : 2 * each]
    table = jnp.concatenate(
        [sta.reshape(-1) * comps, got[:, 2 * each : 3 * each].reshape(-1), got[:, 3 * each :].reshape(-1)]
    )
    stack = detect(extended, panels, table, mine * slabs, mine, slots, comps, height, span, samples)
    return stack.reshape(-1, samples)


def solution(mesh):
    return jax.shard_map(
        per_device,
        mesh=mesh,
        in_specs=(
            P("tpl", None, "slab"),
            P(("tpl", "slab"), None, None, None),
            P(("tpl", "slab"), None),
            P(("tpl", "slab"), None),
            P(("tpl", "slab")),
        ),
        out_specs=P("tpl", "slab"),
        check_vma=False,
    )
```

```python
import functools
import math

import jax
import jax.numpy as jnp
from jax import lax
from jax.experimental import pallas as pl
from jax.experimental.pallas import tpu as pltpu
from jax.sharding import PartitionSpec as P

MAXSHIFT = 256


EPS = 1e-05
MESH = pl.DeviceIdType.MESH


def normalize(templates):
    span = templates.shape[-1]
    rows = templates.astype(jnp.float32)
    centered = rows - jnp.mean(rows, axis=-1, keepdims=True)
    rms = jnp.sqrt(jnp.mean(centered * centered, axis=-1, keepdims=True) + EPS)
    return (centered / (rms * math.sqrt(span))).astype(jnp.bfloat16)


LANES = 128
STEP = 32
TURNS = LANES // STEP
PASS = 4
ROWS = 384
PLANE = 16


def prepare(span, ext_ref, xs_ref, ns_ref, sums_rows):
    rows, width = ext_ref.shape
    block = 256
    reach = block + span
    taps = lax.broadcasted_iota(jnp.int32, (reach, block), 0)
    starts = lax.broadcasted_iota(jnp.int32, (reach, block), 1)
    band = jnp.where((taps >= starts) & (taps < starts + span), 1.0, 0.0).astype(jnp.bfloat16)
    nblocks = (width - span) // block
    root = math.sqrt(span)

    @pl.loop(0, rows // sums_rows)
    def _(step):
        at = pl.ds(pl.multiple_of(step * sums_rows, sums_rows), sums_rows)
        base = pl.multiple_of(step * sums_rows * PLANE, sums_rows * PLANE)
        for row in range(width // LANES):
            xs_ref[pl.ds(base + row, sums_rows, stride=PLANE), :] = ext_ref[at, row * LANES : (row + 1) * LANES].astype(jnp.float32)
        for row in range(width // LANES, PLANE):
            xs_ref[pl.ds(base + row, sums_rows, stride=PLANE), :] = jnp.zeros((sums_rows, LANES), jnp.float32)
        for n in range(nblocks):
            values = ext_ref[at, n * block : n * block + reach]
            wide = values.astype(jnp.float32)
            square = wide * wide
            high = square.astype(jnp.bfloat16)
            low = (square - high.astype(jnp.float32)).astype(jnp.bfloat16)
            sums = jnp.dot(values, band, preferred_element_type=jnp.float32)
            squares = jnp.dot(high, band, preferred_element_type=jnp.float32)
            squares += jnp.dot(low, band, preferred_element_type=jnp.float32)
            spread = (squares - sums * sums / span) / span
            inverse = 1.0 / (root * jnp.sqrt(jnp.maximum(spread, 0.0) + EPS))
            inverse = inverse.astype(jnp.bfloat16).astype(jnp.float32)
            for half in range(block // LANES):
                ns_ref[pl.ds(base + n * (block // LANES) + half, sums_rows, stride=PLANE), :] = inverse[:, half * LANES : (half + 1) * LANES]


def kernel(span, comps, mine, height, slots, table_ref, ext_ref, panels_ref, out_ref, xs_ref, ns_ref, unit_ref, left_ref, right_ref, sum_ref, done_ref, item_ref, where_ref, line_ref):
    prepare(span, ext_ref, xs_ref, ns_ref, ROWS)
    panel = out_ref.shape[0]
    parts = span // LANES
    count = panel * slots

    @pl.loop(0, panels_ref.shape[0] // height)
    def _(step):
        at = pl.ds(pl.multiple_of(step * height, height), height)
        for part in range(parts):
            unit_ref[part, at, :] = panels_ref[at, part * LANES : (part + 1) * LANES].astype(jnp.float32)

    def collect(j, total):
        origin = (j // mine) * height + lax.rem(j, mine) * slots * comps
        base = j * slots

        def one(k, _):
            item_ref[total + k] = base + k
            where_ref[total + k] = j
            line_ref[total + k] = origin + k * comps
            return 0

        live = table_ref[2 * count + j]
        lax.fori_loop(0, live, one, 0)
        sum_ref[j] = jnp.zeros((STEP, LANES), jnp.float32)
        return total + live

    live_slots = lax.fori_loop(0, panel, collect, 0)
    for k in range(PASS - 1):
        item_ref[live_slots + k] = 0
        where_ref[live_slots + k] = panel
        line_ref[live_slots + k] = 0
    sum_ref[panel] = jnp.zeros((STEP, LANES), jnp.float32)

    lane = lax.broadcasted_iota(jnp.int32, (8, LANES), 1)
    lane_wide = lax.broadcasted_iota(jnp.int32, (STEP, LANES), 1)
    lag = lax.broadcasted_iota(jnp.int32, (STEP, LANES), 0)
    inside = lane_wide >= lag
    lane_part = lax.shift_right_logical(lane, 5)
    zero_step = jnp.zeros((STEP, LANES), jnp.float32)
    zero = jnp.zeros((8, LANES), jnp.float32)

    def body(g, _):
        places = []
        for n in range(PASS):
            item = item_ref[g * PASS + n]
            offsets = [table_ref[count + item] + STEP * turn for turn in range(TURNS)]
            firsts = [lax.shift_right_logical(offset, 7) + table_ref[item] * PLANE for offset in offsets]
            rests = [lax.bitwise_and(offset, LANES - 1) for offset in offsets]
            places.append((firsts, rests, line_ref[g * PASS + n]))
        for quad in range(PASS * comps // TURNS):
            for p in range(TURNS):
                n, c = divmod(quad * TURNS + p, comps)
                firsts, rests, origin = places[n]
                i = quad * TURNS + p
                turned = []
                for part in range(parts):
                    line = jnp.broadcast_to(unit_ref[part, pl.ds(origin + c, 1), :], (STEP, LANES))
                    turned.append(pltpu.roll(line, 0, 1, stride=1, stride_axis=0))
                edges = [zero_step] + turned + [zero_step]
                for part in range(parts + 1):
                    piece = jnp.where(inside, edges[part + 1], edges[part])
                    right_ref[i * STEP : (i + 1) * STEP, part * LANES : (part + 1) * LANES] = piece.astype(jnp.bfloat16)
                lines = []
                for turn in range(TURNS):
                    keep = lane >= rests[turn]
                    back = lax.bitwise_and(LANES - rests[turn], LANES - 1)
                    loads = [xs_ref[pl.ds(firsts[turn] + c * PLANE + part, 8), :] for part in range(parts + 2)]
                    lines.append([
                        pltpu.roll(jnp.where(keep, loads[part], loads[part + 1]), back, 1)
                        for part in range(parts + 1)
                    ])
                for part in range(parts + 1):
                    for pair in range(TURNS // 2):
                        both = jnp.concatenate([lines[2 * pair][part], lines[2 * pair + 1][part]], axis=0)
                        at = i * STEP + pair * 16
                        left_ref[at : at + 16, part * LANES : (part + 1) * LANES] = both.astype(jnp.bfloat16)
        products = []
        for quad in range(PASS * comps // TURNS):
            at = slice(quad * LANES, (quad + 1) * LANES)
            products.append(lax.dot_general(
                left_ref[at, :], right_ref[at, :], (((1,), (1,)), ((), ())),
                preferred_element_type=jnp.float32,
            ))
        for n in range(PASS):
            firsts, rests, _ = places[n]
            added = []
            for turn in range(TURNS):
                value = zero
                for c in range(comps):
                    quad, p = divmod(n * comps + c, TURNS)
                    near = ns_ref[pl.ds(firsts[turn] + c * PLANE, 8), :]
                    far = ns_ref[pl.ds(firsts[turn] + c * PLANE + 1, 8), :]
                    back = lax.bitwise_and(LANES + STEP * p - rests[turn], LANES - 1)
                    norm = pltpu.roll(jnp.where(lane >= rests[turn], near, far), back, 1)
                    corr = products[quad][p * STEP + 8 * turn : p * STEP + 8 * turn + 8, :]
                    value = jnp.where(lane_part == p, corr * norm, value)
                added.append(value)
            j = where_ref[g * PASS + n]
            sum_ref[j] += jnp.concatenate(added, axis=0)
        return 0

    lax.fori_loop(0, lax.shift_right_logical(live_slots + PASS - 1, 2), body, 0)

    def finish(j, _):
        value = sum_ref[j]
        value = value + pltpu.roll(value, LANES // 2, 1)
        value = value + pltpu.roll(value, LANES // 4, 1)
        result = zero
        for turn in range(TURNS):
            result = jnp.where(lane_part == turn, value[8 * turn : 8 * turn + 8, :], result)
        used = jnp.full((8, LANES), table_ref[2 * count + j], jnp.int32).astype(jnp.float32)
        result = result * jnp.sqrt(span / (3.0 * used))
        done_ref[pl.ds(pl.multiple_of(j * 8, 8), 8), :] = result
        return 0

    lax.fori_loop(0, panel, finish, 0, unroll=4)
    for block in range(panel // 8):
        for a in range(out_ref.shape[1] // LANES):
            out_ref[block * 8 : block * 8 + 8, a * LANES : (a + 1) * LANES] = done_ref[pl.ds(block * 64 + a, 8, stride=8), :]


def detect(ext, panels, table, panel, mine, slots, comps, height, span, samples):
    smem = pl.BlockSpec(memory_space=pltpu.SMEM)
    vmem = pl.BlockSpec(memory_space=pltpu.VMEM)
    listed = panel * slots + PASS
    held = ext.shape[0] * PLANE * LANES * 8 + panels.size * 6 + ext.size * 2
    return pl.pallas_call(
        functools.partial(kernel, span, comps, mine, height, slots),
        out_shape=jax.ShapeDtypeStruct((panel, samples), jnp.float32),
        in_specs=[smem, vmem, vmem],
        out_specs=vmem,
        scratch_shapes=[
            pltpu.VMEM((ext.shape[0] * PLANE, LANES), jnp.float32),
            pltpu.VMEM((ext.shape[0] * PLANE, LANES), jnp.float32),
            pltpu.VMEM((span // LANES, panels.shape[0], LANES), jnp.float32),
            pltpu.VMEM((PASS * comps * STEP, span + LANES), jnp.bfloat16),
            pltpu.VMEM((PASS * comps * STEP, span + LANES), jnp.bfloat16),
            pltpu.VMEM((panel + 1, STEP, LANES), jnp.float32),
            pltpu.VMEM((panel * 8, LANES), jnp.float32),
            pltpu.SMEM((listed,), jnp.int32),
            pltpu.SMEM((listed,), jnp.int32),
            pltpu.SMEM((listed,), jnp.int32),
        ],
        compiler_params=pltpu.CompilerParams(vmem_limit_bytes=held + (12 << 20)),
    )(table, ext, panels)


def exchange_kernel(reach, data_ref, panel_ref, ext_ref, panels_ref, *sems):
    near_send, near_recv, far_send, far_recv, halo_send, halo_recv = sems[:6]
    wide_send, wide_recv, side_send, side_recv, mate_send, mate_recv = sems[6:]
    rows, samples = data_ref.shape
    height = panel_ref.shape[0]
    slabs = lax.axis_size("slab")
    blocks = lax.axis_size("tpl")
    outer = slabs // 4
    slab = lax.axis_index("slab")
    tpl = lax.axis_index("tpl")
    mate = slab + 1 - 2 * lax.rem(slab, 2)
    side = slab + 2 - 4 * lax.rem(slab // 2, 2)

    barrier = pltpu.get_barrier_semaphore()
    for d in range(1, blocks):
        pl.semaphore_signal(barrier, inc=1, device_id={"tpl": lax.rem(tpl + d, blocks)}, device_id_type=MESH)
    for d in range(1, slabs):
        pl.semaphore_signal(barrier, inc=1, device_id={"slab": lax.rem(slab + d, slabs)}, device_id_type=MESH)
    pl.semaphore_wait(barrier, blocks + slabs - 2)

    def group(t):
        return pl.ds(pl.multiple_of(t * rows, rows), rows)

    def place(p):
        return pl.ds(pl.multiple_of(p * height, height), height)

    def near_copy(d):
        return pltpu.make_async_remote_copy(
            src_ref=data_ref.at[:, :reach], dst_ref=ext_ref.at[group(tpl), :reach],
            send_sem=near_send.at[d], recv_sem=near_recv.at[d],
            device_id={"tpl": lax.rem(tpl + d, blocks)}, device_id_type=MESH)

    def far_copy(d):
        return pltpu.make_async_remote_copy(
            src_ref=data_ref.at[:, reach:], dst_ref=ext_ref.at[group(tpl), reach:samples],
            send_sem=far_send.at[d], recv_sem=far_recv.at[d],
            device_id={"tpl": lax.rem(tpl + d, blocks)}, device_id_type=MESH)

    def halo_copy(d):
        source = data_ref.at[:, :reach]
        if d > 0:
            source = ext_ref.at[group(lax.rem(tpl + blocks - d, blocks)), :reach]
        return pltpu.make_async_remote_copy(
            src_ref=source, dst_ref=ext_ref.at[group(lax.rem(tpl + blocks - d, blocks)), samples:],
            send_sem=halo_send.at[d], recv_sem=halo_recv.at[d],
            device_id={"slab": lax.rem(slab + slabs - 1, slabs)}, device_id_type=MESH)

    def wide_copy(d):
        return pltpu.make_async_remote_copy(
            src_ref=panel_ref, dst_ref=panels_ref.at[place(slab), :],
            send_sem=wide_send.at[d], recv_sem=wide_recv.at[d],
            device_id={"slab": lax.rem(slab + 4 * d, slabs)}, device_id_type=MESH)

    def passed_on(source, owner, send, recv, device):
        return pltpu.make_async_remote_copy(
            src_ref=source, dst_ref=panels_ref.at[place(owner), :],
            send_sem=send, recv_sem=recv, device_id={"slab": device}, device_id_type=MESH)

    def side_copy(d):
        owner = lax.rem(slab + slabs - 4 * d, slabs)
        source = panel_ref if d == 0 else panels_ref.at[place(owner), :]
        return passed_on(source, owner, side_send.at[d], side_recv.at[d], side)

    def mate_copy(d, turn):
        owner = lax.rem((side if turn else slab) + slabs - 4 * d, slabs)
        source = panel_ref if d + turn == 0 else panels_ref.at[place(owner), :]
        at = 2 * d + turn
        return passed_on(source, owner, mate_send.at[at], mate_recv.at[at], mate)

    first = slab == 0
    last = slab == slabs - 1
    for d in range(1, blocks):
        near_copy(d).start()
    for d in range(1, outer):
        wide_copy(d).start()
    for d in range(1, blocks):
        far_copy(d).start()
    side_copy(0).start()
    mate_copy(0, 0).start()

    @pl.when(jnp.logical_not(first))
    def _():
        halo_copy(0).start()

    ext_ref[group(tpl), :samples] = data_ref[...]
    panels_ref[place(slab), :] = panel_ref[...]

    @pl.when(last)
    def _():
        ext_ref[:, samples:] = jnp.zeros((rows * blocks, reach), ext_ref.dtype)

    for d in range(1, outer):
        wide_copy(d).wait_recv()
        side_copy(d).start()
        mate_copy(d, 0).start()
    for d in range(1, blocks):
        near_copy(d).wait_recv()

        @pl.when(jnp.logical_not(first))
        def _():
            halo_copy(d).start()

    for d in range(outer):
        side_copy(d).wait_recv()
        mate_copy(d, 1).start()
    for d in range(1, blocks):
        far_copy(d).wait_recv()
        near_copy(d).wait_send()
        far_copy(d).wait_send()
    for d in range(1, outer):
        wide_copy(d).wait_send()
    for d in range(outer):
        side_copy(d).wait_send()
        for turn in range(2):
            mate_copy(d, turn).wait_recv()
            mate_copy(d, turn).wait_send()

    @pl.when(jnp.logical_not(first))
    def _():
        for d in range(blocks):
            halo_copy(d).wait_send()

    @pl.when(jnp.logical_not(last))
    def _():
        for d in range(blocks):
            halo_copy(d).wait_recv()


def exchange(local, panel, reach):
    slabs = lax.axis_size("slab")
    blocks = lax.axis_size("tpl")
    rows, samples = local.shape
    height, span = panel.shape
    vmem = pl.BlockSpec(memory_space=pltpu.VMEM)
    dma = pltpu.SemaphoreType.DMA
    return pl.pallas_call(
        functools.partial(exchange_kernel, reach),
        out_shape=(
            jax.ShapeDtypeStruct((rows * blocks, samples + reach), local.dtype),
            jax.ShapeDtypeStruct((height * slabs, span), panel.dtype),
        ),
        in_specs=[vmem, vmem],
        out_specs=(vmem, vmem),
        scratch_shapes=[dma((blocks,))] * 6 + [dma((slabs // 4,))] * 4 + [dma((slabs // 2,))] * 2,
        compiler_params=pltpu.CompilerParams(
            collective_id=0, has_side_effects=True, vmem_limit_bytes=16 << 20
        ),
    )(local, panel)


def per_device(data, templates, stations, shifts, used):
    span = templates.shape[3]
    comps = data.shape[1]
    samples = data.shape[2]
    reach = span + MAXSHIFT
    slots = templates.shape[1]
    mine = templates.shape[0]
    local = data.reshape(-1, samples)
    unit = normalize(templates).reshape(-1, span)
    lists = jnp.concatenate(
        [stations.reshape(-1) // 256, stations.reshape(-1) % 256, shifts.reshape(-1), used]
    )
    lists = jnp.pad(lists.astype(jnp.bfloat16), (0, span - lists.shape[0]))
    lists = jnp.pad(lists[None], ((0, 15), (0, 0)))
    extended, panels = exchange(local, jnp.concatenate([unit, lists], axis=0), reach)
    slabs = lax.axis_size("slab")
    height = unit.shape[0] + 16
    each = mine * slots
    got = panels.reshape(slabs, height, span)[:, unit.shape[0], : 3 * each + mine].astype(jnp.int32)
    sta = got[:, :each] * 256 + got[:, each : 2 * each]
    table = jnp.concatenate(
        [sta.reshape(-1) * comps, got[:, 2 * each : 3 * each].reshape(-1), got[:, 3 * each :].reshape(-1)]
    )
    stack = detect(extended, panels, table, mine * slabs, mine, slots, comps, height, span, samples)
    return stack


def solution(mesh):
    return jax.shard_map(
        per_device,
        mesh=mesh,
        in_specs=(
            P("tpl", None, "slab"),
            P(("tpl", "slab"), None, None, None),
            P(("tpl", "slab"), None),
            P(("tpl", "slab"), None),
            P(("tpl", "slab")),
        ),
        out_specs=P("tpl", "slab"),
        check_vma=False,
    )
```

```python
import functools
import math

import jax
import jax.numpy as jnp
from jax import lax
from jax.experimental import pallas as pl
from jax.experimental.pallas import tpu as pltpu
from jax.sharding import PartitionSpec as P

MAXSHIFT = 256


EPS = 1e-05
MESH = pl.DeviceIdType.MESH


def normalize(templates):
    span = templates.shape[-1]
    rows = templates.astype(jnp.float32)
    centered = rows - jnp.mean(rows, axis=-1, keepdims=True)
    rms = jnp.sqrt(jnp.mean(centered * centered, axis=-1, keepdims=True) + EPS)
    return (centered / (rms * math.sqrt(span))).astype(jnp.bfloat16)


LANES = 128
STEP = 32
TURNS = LANES // STEP
PASS = 4
ROWS = 384
PLANE = 16


def prepare(span, ext_ref, xs_ref, ns_ref, sums_rows):
    rows, width = ext_ref.shape
    block = 256
    reach = block + span
    taps = lax.broadcasted_iota(jnp.int32, (reach, block), 0)
    starts = lax.broadcasted_iota(jnp.int32, (reach, block), 1)
    band = jnp.where((taps >= starts) & (taps < starts + span), 1.0, 0.0).astype(jnp.bfloat16)
    nblocks = (width - span) // block
    root = math.sqrt(span)

    @pl.loop(0, rows // sums_rows)
    def _(step):
        at = pl.ds(pl.multiple_of(step * sums_rows, sums_rows), sums_rows)
        base = pl.multiple_of(step * sums_rows * PLANE, sums_rows * PLANE)
        for row in range(width // LANES):
            xs_ref[pl.ds(base + row, sums_rows, stride=PLANE), :] = ext_ref[at, row * LANES : (row + 1) * LANES].astype(jnp.float32)
        for row in range(width // LANES, PLANE):
            xs_ref[pl.ds(base + row, sums_rows, stride=PLANE), :] = jnp.zeros((sums_rows, LANES), jnp.float32)
        for n in range(nblocks):
            values = ext_ref[at, n * block : n * block + reach]
            wide = values.astype(jnp.float32)
            square = wide * wide
            high = square.astype(jnp.bfloat16)
            low = (square - high.astype(jnp.float32)).astype(jnp.bfloat16)
            sums = jnp.dot(values, band, preferred_element_type=jnp.float32)
            squares = jnp.dot(high, band, preferred_element_type=jnp.float32)
            squares += jnp.dot(low, band, preferred_element_type=jnp.float32)
            spread = (squares - sums * sums / span) / span
            inverse = 1.0 / (root * jnp.sqrt(jnp.maximum(spread, 0.0) + EPS))
            inverse = inverse.astype(jnp.bfloat16).astype(jnp.float32)
            for half in range(block // LANES):
                ns_ref[pl.ds(base + n * (block // LANES) + half, sums_rows, stride=PLANE), :] = inverse[:, half * LANES : (half + 1) * LANES]


def kernel(span, comps, hop, mine, height, slots, table_ref, ext_ref, panels_ref, out_ref, xs_ref, ns_ref, unit_ref, left_ref, right_ref, sum_ref, done_ref, item_ref, where_ref, line_ref):
    prepare(span, ext_ref, xs_ref, ns_ref, ROWS)
    panel = out_ref.shape[0]
    parts = span // LANES
    count = panel * slots

    @pl.loop(0, panels_ref.shape[0] // height)
    def _(step):
        at = pl.ds(pl.multiple_of(step * height, height), height)
        for part in range(parts):
            unit_ref[part, at, :] = panels_ref[at, part * LANES : (part + 1) * LANES].astype(jnp.float32)

    def collect(j, total):
        origin = (j // mine) * height + lax.rem(j, mine) * slots * comps
        base = j * slots

        def one(k, _):
            item_ref[total + k] = base + k
            where_ref[total + k] = j
            line_ref[total + k] = origin + k * comps
            return 0

        live = table_ref[2 * count + j]
        lax.fori_loop(0, live, one, 0)
        sum_ref[j] = jnp.zeros((STEP, LANES), jnp.float32)
        return total + live

    live_slots = lax.fori_loop(0, panel, collect, 0)
    for k in range(PASS - 1):
        item_ref[live_slots + k] = 0
        where_ref[live_slots + k] = panel
        line_ref[live_slots + k] = 0
    sum_ref[panel] = jnp.zeros((STEP, LANES), jnp.float32)

    lane = lax.broadcasted_iota(jnp.int32, (8, LANES), 1)
    lane_wide = lax.broadcasted_iota(jnp.int32, (STEP, LANES), 1)
    lag = lax.broadcasted_iota(jnp.int32, (STEP, LANES), 0)
    inside = lane_wide >= lag
    lane_part = lax.shift_right_logical(lane, 5)
    zero_step = jnp.zeros((STEP, LANES), jnp.float32)
    zero = jnp.zeros((8, LANES), jnp.float32)

    def body(g, _):
        places = []
        for n in range(PASS):
            item = item_ref[g * PASS + n]
            offsets = [table_ref[count + item] + STEP * turn for turn in range(TURNS)]
            firsts = [lax.shift_right_logical(offset, 7) + table_ref[item] * PLANE for offset in offsets]
            rests = [lax.bitwise_and(offset, LANES - 1) for offset in offsets]
            places.append((firsts, rests, line_ref[g * PASS + n]))
        for quad in range(PASS * comps // TURNS):
            for p in range(TURNS):
                n, c = divmod(quad * TURNS + p, comps)
                firsts, rests, origin = places[n]
                i = quad * TURNS + p
                turned = []
                for part in range(parts):
                    line = jnp.broadcast_to(unit_ref[part, pl.ds(origin + c, 1), :], (STEP, LANES))
                    turned.append(pltpu.roll(line, 0, 1, stride=1, stride_axis=0))
                edges = [zero_step] + turned + [zero_step]
                for part in range(parts + 1):
                    piece = jnp.where(inside, edges[part + 1], edges[part])
                    right_ref[i * STEP : (i + 1) * STEP, part * LANES : (part + 1) * LANES] = piece.astype(jnp.bfloat16)
                lines = []
                for turn in range(TURNS):
                    keep = lane >= rests[turn]
                    back = lax.bitwise_and(LANES - rests[turn], LANES - 1)
                    loads = [xs_ref[pl.ds(firsts[turn] + c * hop * PLANE + part, 8), :] for part in range(parts + 2)]
                    lines.append([
                        pltpu.roll(jnp.where(keep, loads[part], loads[part + 1]), back, 1)
                        for part in range(parts + 1)
                    ])
                for part in range(parts + 1):
                    for pair in range(TURNS // 2):
                        both = jnp.concatenate([lines[2 * pair][part], lines[2 * pair + 1][part]], axis=0)
                        at = i * STEP + pair * 16
                        left_ref[at : at + 16, part * LANES : (part + 1) * LANES] = both.astype(jnp.bfloat16)
        products = []
        for quad in range(PASS * comps // TURNS):
            at = slice(quad * LANES, (quad + 1) * LANES)
            products.append(lax.dot_general(
                left_ref[at, :], right_ref[at, :], (((1,), (1,)), ((), ())),
                preferred_element_type=jnp.float32,
            ))
        for n in range(PASS):
            firsts, rests, _ = places[n]
            added = []
            for turn in range(TURNS):
                value = zero
                for c in range(comps):
                    quad, p = divmod(n * comps + c, TURNS)
                    near = ns_ref[pl.ds(firsts[turn] + c * hop * PLANE, 8), :]
                    far = ns_ref[pl.ds(firsts[turn] + c * hop * PLANE + 1, 8), :]
                    back = lax.bitwise_and(LANES + STEP * p - rests[turn], LANES - 1)
                    norm = pltpu.roll(jnp.where(lane >= rests[turn], near, far), back, 1)
                    corr = products[quad][p * STEP + 8 * turn : p * STEP + 8 * turn + 8, :]
                    value = jnp.where(lane_part == p, corr * norm, value)
                added.append(value)
            j = where_ref[g * PASS + n]
            sum_ref[j] += jnp.concatenate(added, axis=0)
        return 0

    lax.fori_loop(0, lax.shift_right_logical(live_slots + PASS - 1, 2), body, 0)

    def finish(j, _):
        value = sum_ref[j]
        value = value + pltpu.roll(value, LANES // 2, 1)
        value = value + pltpu.roll(value, LANES // 4, 1)
        result = zero
        for turn in range(TURNS):
            result = jnp.where(lane_part == turn, value[8 * turn : 8 * turn + 8, :], result)
        used = jnp.full((8, LANES), table_ref[2 * count + j], jnp.int32).astype(jnp.float32)
        result = result * jnp.sqrt(span / (3.0 * used))
        done_ref[pl.ds(pl.multiple_of(j * 8, 8), 8), :] = result
        return 0

    lax.fori_loop(0, panel, finish, 0, unroll=4)
    for block in range(panel // 8):
        for a in range(out_ref.shape[1] // LANES):
            out_ref[block * 8 : block * 8 + 8, a * LANES : (a + 1) * LANES] = done_ref[pl.ds(block * 64 + a, 8, stride=8), :]


def detect(ext, panels, table, panel, mine, slots, comps, hop, height, span, samples):
    smem = pl.BlockSpec(memory_space=pltpu.SMEM)
    vmem = pl.BlockSpec(memory_space=pltpu.VMEM)
    listed = panel * slots + PASS
    held = ext.shape[0] * PLANE * LANES * 8 + panels.size * 6 + ext.size * 2
    return pl.pallas_call(
        functools.partial(kernel, span, comps, hop, mine, height, slots),
        out_shape=jax.ShapeDtypeStruct((panel, samples), jnp.float32),
        in_specs=[smem, vmem, vmem],
        out_specs=vmem,
        scratch_shapes=[
            pltpu.VMEM((ext.shape[0] * PLANE, LANES), jnp.float32),
            pltpu.VMEM((ext.shape[0] * PLANE, LANES), jnp.float32),
            pltpu.VMEM((span // LANES, panels.shape[0], LANES), jnp.float32),
            pltpu.VMEM((PASS * comps * STEP, span + LANES), jnp.bfloat16),
            pltpu.VMEM((PASS * comps * STEP, span + LANES), jnp.bfloat16),
            pltpu.VMEM((panel + 1, STEP, LANES), jnp.float32),
            pltpu.VMEM((panel * 8, LANES), jnp.float32),
            pltpu.SMEM((listed,), jnp.int32),
            pltpu.SMEM((listed,), jnp.int32),
            pltpu.SMEM((listed,), jnp.int32),
        ],
        compiler_params=pltpu.CompilerParams(vmem_limit_bytes=held + (12 << 20)),
    )(table, ext, panels)


def exchange_kernel(reach, data_ref, panel_ref, ext_ref, panels_ref, *sems):
    near_send, near_recv, far_send, far_recv, halo_send, halo_recv = sems[:6]
    wide_send, wide_recv, side_send, side_recv, mate_send, mate_recv = sems[6:]
    rows, samples = data_ref.shape
    height = panel_ref.shape[0]
    slabs = lax.axis_size("slab")
    blocks = lax.axis_size("tpl")
    outer = slabs // 4
    slab = lax.axis_index("slab")
    tpl = lax.axis_index("tpl")
    mate = slab + 1 - 2 * lax.rem(slab, 2)
    side = slab + 2 - 4 * lax.rem(slab // 2, 2)

    barrier = pltpu.get_barrier_semaphore()
    for d in range(1, blocks):
        pl.semaphore_signal(barrier, inc=1, device_id={"tpl": lax.rem(tpl + d, blocks)}, device_id_type=MESH)
    for d in range(1, slabs):
        pl.semaphore_signal(barrier, inc=1, device_id={"slab": lax.rem(slab + d, slabs)}, device_id_type=MESH)
    pl.semaphore_wait(barrier, blocks + slabs - 2)

    def group(t):
        return pl.ds(pl.multiple_of(t * rows, rows), rows)

    def place(p):
        return pl.ds(pl.multiple_of(p * height, height), height)

    def near_copy(d):
        return pltpu.make_async_remote_copy(
            src_ref=data_ref.at[:, :reach], dst_ref=ext_ref.at[group(tpl), :reach],
            send_sem=near_send.at[d], recv_sem=near_recv.at[d],
            device_id={"tpl": lax.rem(tpl + d, blocks)}, device_id_type=MESH)

    def far_copy(d):
        return pltpu.make_async_remote_copy(
            src_ref=data_ref.at[:, reach:], dst_ref=ext_ref.at[group(tpl), reach:samples],
            send_sem=far_send.at[d], recv_sem=far_recv.at[d],
            device_id={"tpl": lax.rem(tpl + d, blocks)}, device_id_type=MESH)

    def halo_copy(d):
        source = data_ref.at[:, :reach]
        if d > 0:
            source = ext_ref.at[group(lax.rem(tpl + blocks - d, blocks)), :reach]
        return pltpu.make_async_remote_copy(
            src_ref=source, dst_ref=ext_ref.at[group(lax.rem(tpl + blocks - d, blocks)), samples:],
            send_sem=halo_send.at[d], recv_sem=halo_recv.at[d],
            device_id={"slab": lax.rem(slab + slabs - 1, slabs)}, device_id_type=MESH)

    def wide_copy(d):
        return pltpu.make_async_remote_copy(
            src_ref=panel_ref, dst_ref=panels_ref.at[place(slab), :],
            send_sem=wide_send.at[d], recv_sem=wide_recv.at[d],
            device_id={"slab": lax.rem(slab + 4 * d, slabs)}, device_id_type=MESH)

    def passed_on(source, owner, send, recv, device):
        return pltpu.make_async_remote_copy(
            src_ref=source, dst_ref=panels_ref.at[place(owner), :],
            send_sem=send, recv_sem=recv, device_id={"slab": device}, device_id_type=MESH)

    def side_copy(d):
        owner = lax.rem(slab + slabs - 4 * d, slabs)
        source = panel_ref if d == 0 else panels_ref.at[place(owner), :]
        return passed_on(source, owner, side_send.at[d], side_recv.at[d], side)

    def mate_copy(d, turn):
        owner = lax.rem((side if turn else slab) + slabs - 4 * d, slabs)
        source = panel_ref if d + turn == 0 else panels_ref.at[place(owner), :]
        at = 2 * d + turn
        return passed_on(source, owner, mate_send.at[at], mate_recv.at[at], mate)

    first = slab == 0
    last = slab == slabs - 1
    for d in range(1, blocks):
        near_copy(d).start()
    for d in range(1, outer):
        wide_copy(d).start()
    for d in range(1, blocks):
        far_copy(d).start()
    side_copy(0).start()
    mate_copy(0, 0).start()

    @pl.when(jnp.logical_not(first))
    def _():
        halo_copy(0).start()

    ext_ref[group(tpl), :samples] = data_ref[...]
    panels_ref[place(slab), :] = panel_ref[...]

    @pl.when(last)
    def _():
        ext_ref[:, samples:] = jnp.zeros((rows * blocks, reach), ext_ref.dtype)

    for d in range(1, outer):
        wide_copy(d).wait_recv()
        side_copy(d).start()
        mate_copy(d, 0).start()
    for d in range(1, blocks):
        near_copy(d).wait_recv()

        @pl.when(jnp.logical_not(first))
        def _():
            halo_copy(d).start()

    for d in range(outer):
        side_copy(d).wait_recv()
        mate_copy(d, 1).start()
    for d in range(1, blocks):
        far_copy(d).wait_recv()
        near_copy(d).wait_send()
        far_copy(d).wait_send()
    for d in range(1, outer):
        wide_copy(d).wait_send()
    for d in range(outer):
        side_copy(d).wait_send()
        for turn in range(2):
            mate_copy(d, turn).wait_recv()
            mate_copy(d, turn).wait_send()

    @pl.when(jnp.logical_not(first))
    def _():
        for d in range(blocks):
            halo_copy(d).wait_send()

    @pl.when(jnp.logical_not(last))
    def _():
        for d in range(blocks):
            halo_copy(d).wait_recv()


def exchange(local, panel, reach):
    slabs = lax.axis_size("slab")
    blocks = lax.axis_size("tpl")
    rows, samples = local.shape
    height, span = panel.shape
    vmem = pl.BlockSpec(memory_space=pltpu.VMEM)
    dma = pltpu.SemaphoreType.DMA
    return pl.pallas_call(
        functools.partial(exchange_kernel, reach),
        out_shape=(
            jax.ShapeDtypeStruct((rows * blocks, samples + reach), local.dtype),
            jax.ShapeDtypeStruct((height * slabs, span), panel.dtype),
        ),
        in_specs=[vmem, vmem],
        out_specs=(vmem, vmem),
        scratch_shapes=[dma((blocks,))] * 6 + [dma((slabs // 4,))] * 4 + [dma((slabs // 2,))] * 2,
        compiler_params=pltpu.CompilerParams(
            collective_id=0, has_side_effects=True, vmem_limit_bytes=16 << 20
        ),
    )(local, panel)


def per_device(data, templates, stations, shifts, used):
    span = templates.shape[3]
    comps = data.shape[1]
    samples = data.shape[2]
    reach = span + MAXSHIFT
    slots = templates.shape[1]
    mine = templates.shape[0]
    hop = data.shape[0]
    local = jnp.transpose(data, (1, 0, 2)).reshape(-1, samples)
    unit = normalize(templates).reshape(-1, span)
    lists = jnp.concatenate(
        [stations.reshape(-1) // 256, stations.reshape(-1) % 256, shifts.reshape(-1), used]
    )
    lists = jnp.pad(lists.astype(jnp.bfloat16), (0, span - lists.shape[0]))
    lists = jnp.pad(lists[None], ((0, 15), (0, 0)))
    extended, panels = exchange(local, jnp.concatenate([unit, lists], axis=0), reach)
    slabs = lax.axis_size("slab")
    height = unit.shape[0] + 16
    each = mine * slots
    got = panels.reshape(slabs, height, span)[:, unit.shape[0], : 3 * each + mine].astype(jnp.int32)
    sta = got[:, :each] * 256 + got[:, each : 2 * each]
    table = jnp.concatenate(
        [(sta // hop * (hop * comps) + sta % hop).reshape(-1), got[:, 2 * each : 3 * each].reshape(-1), got[:, 3 * each :].reshape(-1)]
    )
    stack = detect(extended, panels, table, mine * slabs, mine, slots, comps, hop, height, span, samples)
    return stack


def solution(mesh):
    return jax.shard_map(
        per_device,
        mesh=mesh,
        in_specs=(
            P("tpl", None, "slab"),
            P(("tpl", "slab"), None, None, None),
            P(("tpl", "slab"), None),
            P(("tpl", "slab"), None),
            P(("tpl", "slab")),
        ),
        out_specs=P("tpl", "slab"),
        check_vma=False,
    )
```
